32 devices in a mesh: prow: 8 (over z, y), pcol: 4 (over x, core).
Axes of the slice: x: 2, y: 2, z: 4, core: 2. Of those that a mesh axis runs over, the one named last changes fastest.
Arguments:
- b_panel: float32 [1024, 512], P('prow'), may hold values from -6 to 6
- b_rest: float32 [8192, 512], P('prow'), may hold values from -6 to 6
- u_diag: float32 [1024, 1024], P('prow', 'pcol'), as said below
- u_panel: float32 [1024, 8192], P('pcol', 'prow'), may hold values from -0.1875 to 0.1875
- l_diag: float32 [1024, 1024], P('prow', 'pcol'), as said below
- l_below: float32 [8192, 1024], P('prow', 'pcol'), may hold values from -0.09375 to 0.09375
- v_below: float32 [8192, 512], P('prow'), may hold values from -6 to 6
- pivot: int32 [1024], replicated, may hold values from 0 to 8191, as said below
Outputs:
- w_rest: float32 [8192, 512], P('prow')
- x_panel: float32 [1024, 512], P('prow')
- x_rest: float32 [8192, 512], P('prow')
The draws below stay inside these ranges and needn't reach their ends.
Inputs may be any that keep to these rules, and one draw needn't show every extreme that they name: `pivot`: the 1024 entries are distinct, so the interchanges are disjoint. `u_diag`: upper triangular; its diagonal lies in 1 to 2. `l_diag`: lower triangular; its diagonal is one.
All inputs are finite; a program needn't handle non-finite values.
Results may differ from the reference program's by a relative error of at most 0.00007.
Values sent between devices are 32-bit elements; how exact they have to be, the bound alone decides.
A program may use at most 128 MiB of HBM per device.

```python
import jax
import jax.numpy as jnp
from jax import lax

NB = 1024
RHS = 512
ROWS_DEV = 1024
ROWS = 8192
N_PROW = 8


def draw_u_diag(key, part):
    first_key, second_key = jax.random.split(key)
    spread = 0.5 * jax.random.normal(first_key, (NB, NB), jnp.float32) / jnp.sqrt(jnp.float32(NB))
    diag_vals = jax.random.uniform(second_key, (NB,), jnp.float32, 1.0, 2.0)
    row_index = jnp.arange(NB)[:, None]
    col_index = jnp.arange(NB)[None, :]
    upper = jnp.where(col_index > row_index, spread, 0.0)
    return upper + jnp.where(col_index == row_index, diag_vals[:, None], 0.0)


def draw_l_diag(key, part):
    spread = 0.5 * jax.random.normal(key, (NB, NB), jnp.float32) / jnp.sqrt(jnp.float32(NB))
    row_index = jnp.arange(NB)[:, None]
    col_index = jnp.arange(NB)[None, :]
    lower = jnp.where(col_index < row_index, spread, 0.0)
    return lower + jnp.where(col_index == row_index, 1.0, 0.0)


def draw_pivot(key, part):
    group = NB // N_PROW
    clustered = N_PROW // 4
    key_src, key_dst, key_off, key_rest = jax.random.split(key, 4)
    sources = (jax.random.permutation(key_src, N_PROW - 2) + 1).astype(jnp.int32)[:clustered]
    targets = jax.random.permutation(key_dst, N_PROW).astype(jnp.int32)[:clustered]
    offsets = jax.random.randint(key_off, (clustered,), 0, ROWS_DEV - group + 1).astype(jnp.int32)
    shuffled = (jax.random.permutation(key_rest, ROWS - 2) + 1).astype(jnp.int32)
    row_source = shuffled // ROWS_DEV
    taken = jnp.any(row_source[:, None] == sources[None, :], axis=1).astype(jnp.int32)
    order = jnp.argsort(taken, stable=True)
    head = jnp.array([ROWS - 1, 0], jnp.int32)
    pool = jnp.concatenate([head, shuffled[order]]).astype(jnp.int32)
    panel_index = jnp.arange(NB, dtype=jnp.int32)
    target_of = panel_index // group
    match = target_of[:, None] == targets[None, :]
    is_clustered = jnp.any(match, axis=1)
    run_start = jnp.sum(jnp.where(match, sources[None, :] * ROWS_DEV + offsets[None, :], 0), axis=1).astype(jnp.int32)
    cluster_row = run_start + panel_index % group
    free_rank = (jnp.cumsum(1 - is_clustered.astype(jnp.int32)) - 1).astype(jnp.int32)
    free_row = pool[jnp.clip(free_rank, 0, NB - 1).astype(jnp.int32)]
    return jnp.where(is_clustered, cluster_row, free_row).astype(jnp.int32)


def spiked(drawn, rng, source, target, parts, factor):
    owner, partner = [(jnp.arange(drawn.shape[dim]) // (drawn.shape[dim] // parts)).reshape([-1 if axis == dim else 1 for axis in range(drawn.ndim)]) for dim in (source, target)]
    chosen = jax.random.permutation(rng, parts)[partner]
    strong = (owner == chosen) | (owner == (partner + parts // 2) % parts)
    return jnp.where(strong, factor * drawn, drawn)


def block_levels(stream_key, shape, cuts, low, top_value):
    gain = 1.0
    for dim, shards_of in cuts:
        heights = jax.random.uniform(jax.random.fold_in(jax.random.fold_in(stream_key, 6), dim), (shards_of,), jnp.float32, low / len(cuts), top_value / len(cuts))
        gain = gain * jnp.repeat(jnp.exp(heights), shape[dim] // shards_of).reshape((-1,) + (1,) * (len(shape) - 1 - dim))
    return gain


def gaussian(rng, shape, scale, bound, shards=(), held_as=jnp.bfloat16):
    entries = scale * jax.random.normal(rng, shape, jnp.float32)
    if shards:
        entries = entries * block_levels(rng, shape, shards, -0.22, 0.18)
    return jnp.clip(entries, -bound, bound).astype(held_as)


def heavy_noise(own_key, dims, width, limit, shards, heavy, kind=jnp.bfloat16):
    drawn = width * jax.random.normal(own_key, dims, jnp.float32)
    if shards:
        drawn = drawn * block_levels(own_key, dims, shards, -0.22, 0.18)
    return jnp.clip(spiked(drawn, jax.random.fold_in(own_key, 3), *heavy), -limit, limit).astype(kind)


def setup_inputs(seed: int = 0) -> dict:
    keys = jax.random.split(jax.random.key(seed), 9)
    b_panel = gaussian(keys[0], (NB, RHS), 1.0, 6.0, ((0, 8),), jnp.float32)
    b_rest = gaussian(keys[1], (ROWS, RHS), 1.0, 6.0, ((0, 8),), jnp.float32)
    u_diag = draw_u_diag(jax.random.fold_in(keys[8], 71), 0)
    u_panel = gaussian(keys[3], (NB, ROWS), NB ** -0.5, 0.1875, ((0, 4), (1, 8)), jnp.float32)
    l_diag = draw_l_diag(jax.random.fold_in(keys[8], 71), 0)
    l_below = heavy_noise(keys[5], (ROWS, NB), ROWS ** -0.5, 0.09375, ((0, 8), (1, 4)), (0, 1, 8, 2.0), jnp.float32)
    v_below = gaussian(keys[6], (ROWS, RHS), 1.0, 6.0, ((0, 8),), jnp.float32)
    pivot = draw_pivot(jax.random.fold_in(keys[8], 71), 0)
    return dict(b_panel=b_panel, b_rest=b_rest, u_diag=u_diag, u_panel=u_panel, l_diag=l_diag, l_below=l_below, v_below=v_below, pivot=pivot)


def reference(b_panel, b_rest, u_diag, u_panel, l_diag, l_below, v_below, pivot):
    highest = lax.Precision.HIGHEST
    w_panel = lax.linalg.triangular_solve(u_diag, b_panel, left_side=True, lower=False, transpose_a=True)
    update = lax.dot_general(u_panel.astype(jnp.float32), w_panel.astype(jnp.float32), (((0,), (0,)), ((), ())), precision=highest, preferred_element_type=jnp.float32)
    w_rest = b_rest - update
    coupling = lax.dot_general(l_below.astype(jnp.float32), v_below.astype(jnp.float32), (((0,), (0,)), ((), ())), precision=highest, preferred_element_type=jnp.float32)
    v_panel = lax.linalg.triangular_solve(l_diag, w_panel - coupling, left_side=True, lower=True, transpose_a=True, unit_diagonal=True)
    x_panel = v_below[pivot]
    x_rest = v_below.at[pivot].set(v_panel)
    return (w_rest, x_panel, x_rest)
```

```python
import functools

import jax
import jax.numpy as jnp
from jax import lax
from jax.experimental import pallas as pl
from jax.experimental.pallas import tpu as pltpu
from jax.sharding import PartitionSpec as P

F32 = jnp.float32
BF16 = jnp.bfloat16
NN = (((1,), (0,)), ((), ()))
TN = (((0,), (0,)), ((), ()))
NT = (((1,), (1,)), ((), ()))
BLOCK = 128


def split(x):
    high = x.astype(BF16)
    return high, (x - high.astype(F32)).astype(BF16)


def dot(left, right, dims):
    return lax.dot_general(left, right, dims, preferred_element_type=F32)


def dot3(left, right, dims=NN):
    (lh, ll), (rh, rl) = left, right
    return dot(lh, rh, dims) + (dot(lh, rl, dims) + dot(ll, rh, dims))


def inverse(square, upper):
    size = square.shape[0]
    row = lax.broadcasted_iota(jnp.int32, (size, size), 0)
    col = lax.broadcasted_iota(jnp.int32, (size, size), 1)
    eye = jnp.where(row == col, 1.0, 0.0)
    if upper:
        on_diag = jnp.where(row == col, square, 0.0)
        strict = jnp.where(col > row, square, 0.0) / jnp.sum(on_diag, axis=1, keepdims=True)
    else:
        strict = jnp.where(col < row, square, 0.0)
    result = eye - strict
    halves = split(strict)
    power = dot3(halves, halves)
    reach = 2
    while reach < size:
        halves = split(power)
        result = result + dot3(split(result), halves)
        reach *= 2
        if reach < size:
            power = dot3(halves, halves)
    if upper:
        result = result / jnp.sum(on_diag, axis=0, keepdims=True)
    return result


def prep_kernel(pre, u_ref, l_ref, b_ref, lb_ref, vb_ref, piv_ref, pack_ref, coup_ref, pick_ref):
    i = lax.axis_index("prow")
    j = lax.axis_index("pcol")
    cols = u_ref.shape[1]
    chunk = pick_ref.shape[1]
    mine = pl.ds(pl.multiple_of(j * chunk, chunk), chunk)
    pack_ref[:, :cols] = u_ref[...]
    pack_ref[:, cols : 2 * cols] = l_ref[...]
    pack_ref[:, 2 * cols :] = b_ref[:, mine]
    if pre:
        ratio = cols // BLOCK

        @pl.when(i // ratio == j)
        def _():
            at = pl.multiple_of((i % ratio) * BLOCK, BLOCK)
            pack_ref[:, pl.ds(at, BLOCK)] = inverse(u_ref[:, pl.ds(at, BLOCK)], True)
            pack_ref[:, pl.ds(cols + at, BLOCK)] = inverse(l_ref[:, pl.ds(at, BLOCK)], False)

    coup_ref[...] = dot3(split(vb_ref[...]), split(lb_ref[...]), TN)
    rows = vb_ref.shape[0]
    total = piv_ref.shape[1]
    local = piv_ref[...] - i * rows
    hot = jnp.where(lax.broadcasted_iota(jnp.int32, (rows, total), 0) == local, 1.0, 0.0).astype(BF16)
    part = vb_ref[:, mine]
    first, rest = split(part)
    second = (part - first.astype(F32)).astype(BF16)
    third = (part - first.astype(F32) - second.astype(F32)).astype(BF16)
    pick_ref[...] = dot(hot, first, TN) + dot(hot, second, TN) + dot(hot, third, TN)


def main_kernel(pre, n_row, n_col, g_ref, c_ref, up_ref, br_ref, vb_ref, piv_ref, wr_ref, xr_ref, uh, ul, lh, ll, bs, cs, wh, wl):
    i = lax.axis_index("prow")
    rows = g_ref.shape[1]
    cols = up_ref.shape[0] // n_col
    chunk = g_ref.shape[2] - 2 * cols
    crow = c_ref.shape[1]
    total = uh.shape[0]
    for a in range(n_row):
        for b in range(n_col):
            at = a * n_col + b
            rs = slice(a * rows, (a + 1) * rows)
            cs_ = slice(b * cols, (b + 1) * cols)
            if a * rows < (b + 1) * cols:
                uh[rs, cs_], ul[rs, cs_] = split(g_ref[at, :, :cols])
            if (a + 1) * rows > b * cols:
                lh[rs, cs_], ll[rs, cs_] = split(g_ref[at, :, cols : 2 * cols])
            bs[rs, b * chunk : (b + 1) * chunk] = g_ref[at, :, 2 * cols :]
            cs[a * crow : (a + 1) * crow, cs_] = c_ref[at]
    count = total // BLOCK
    if not pre:
        for p in range(count):
            sl = slice(p * BLOCK, (p + 1) * BLOCK)
            uh[sl, sl], ul[sl, sl] = split(inverse(uh[sl, sl].astype(F32) + ul[sl, sl].astype(F32), True))
            lh[sl, sl], ll[sl, sl] = split(inverse(lh[sl, sl].astype(F32) + ll[sl, sl].astype(F32), False))
    for p in range(count):
        first = p * BLOCK
        sl = slice(first, first + BLOCK)
        rhs = bs[sl, :].T
        if p:
            rhs = rhs - dot3((wh[:, :first], wl[:, :first]), (uh[:first, sl], ul[:first, sl]))
        out = dot3(split(rhs), (uh[sl, sl], ul[sl, sl]))
        cs[:, sl] = out - cs[:, sl]
        wh[:, sl], wl[:, sl] = split(out)
    tile = 256
    for t in range(up_ref.shape[1] // tile):
        ts = slice(t * tile, (t + 1) * tile)
        update = dot3((wh[...], wl[...]), split(up_ref[:, ts]))
        wr_ref[ts, :] = br_ref[ts, :] - update.T
    for p in reversed(range(count)):
        first = p * BLOCK
        last = first + BLOCK
        sl = slice(first, last)
        rhs = cs[:, sl]
        if last < total:
            rhs = rhs - dot3((wh[:, last:], wl[:, last:]), (lh[last:, sl], ll[last:, sl]))
        out = dot3(split(rhs), (lh[sl, sl], ll[sl, sl]))
        cs[:, sl] = out
        wh[:, sl], wl[:, sl] = split(out)
    all_rows = vb_ref.shape[0]
    for t in range(all_rows // tile):
        ts = slice(t * tile, (t + 1) * tile)
        local = piv_ref[...] - (i * all_rows + t * tile)
        hit = lax.broadcasted_iota(jnp.int32, (tile, total), 0) == local
        hot = jnp.where(hit, 1.0, 0.0)
        used = jnp.sum(hot, axis=1, keepdims=True) > 0.5
        hot = hot.astype(BF16)
        new = dot(hot, wh[...], NT) + dot(hot, wl[...], NT)
        xr_ref[ts, :] = jnp.where(used, new, vb_ref[ts, :])


def body(n_row, n_col, b_panel, b_rest, u_diag, u_panel, l_diag, l_below, v_below, pivot):
    rows, cols = u_diag.shape
    total, rhs = pivot.shape[0], b_panel.shape[1]
    chunk = rhs // n_col
    pre = rows == BLOCK
    piv = pivot[None, :]
    vm = pl.BlockSpec(memory_space=pltpu.VMEM)
    params = pltpu.CompilerParams(vmem_limit_bytes=56 << 20)
    pack, coup, pick = pl.pallas_call(
        functools.partial(prep_kernel, pre),
        out_shape=(
            jax.ShapeDtypeStruct((rows, 2 * cols + chunk), F32),
            jax.ShapeDtypeStruct((rhs, cols), F32),
            jax.ShapeDtypeStruct((total, chunk), F32),
        ),
        in_specs=[vm] * 6,
        out_specs=(vm, vm, vm),
        compiler_params=params,
    )(u_diag, l_diag, b_panel, l_below, v_below, piv)
    gathered = lax.all_gather(pack, ("prow", "pcol"), axis=0)
    upan = lax.all_gather(u_panel, "pcol", axis=0, tiled=True)
    csum = lax.psum_scatter(coup, "prow", scatter_dimension=0, tiled=True)
    call = lax.all_gather(csum, ("prow", "pcol"), axis=0)
    xsum = lax.psum_scatter(pick, "prow", scatter_dimension=0, tiled=True)
    x_panel = lax.all_gather(xsum, "pcol", axis=1, tiled=True)
    w_rest, x_rest = pl.pallas_call(
        functools.partial(main_kernel, pre, n_row, n_col),
        out_shape=(jax.ShapeDtypeStruct(b_rest.shape, F32), jax.ShapeDtypeStruct(v_below.shape, F32)),
        in_specs=[vm] * 6,
        out_specs=(vm, vm),
        scratch_shapes=[pltpu.VMEM((total, total), BF16)] * 4
        + [pltpu.VMEM((total, rhs), F32), pltpu.VMEM((rhs, total), F32)]
        + [pltpu.VMEM((rhs, total), BF16)] * 2,
        compiler_params=params,
    )(gathered, call, upan, b_rest, v_below, piv)
    return w_rest, x_panel, x_rest


def solution(mesh):
    in_specs = (
        P("prow", None),
        P("prow", None),
        P("prow", "pcol"),
        P("pcol", "prow"),
        P("prow", "pcol"),
        P("prow", "pcol"),
        P("prow", None),
        P(),
    )
    out_specs = (P("prow", None), P("prow", None), P("prow", None))
    step = functools.partial(body, mesh.shape["prow"], mesh.shape["pcol"])
    return jax.shard_map(step, mesh=mesh, in_specs=in_specs, out_specs=out_specs, check_vma=False)
```

```python
import functools

import jax
import jax.numpy as jnp
from jax import lax
from jax.experimental import pallas as pl
from jax.experimental.pallas import tpu as pltpu
from jax.sharding import PartitionSpec as P

F32 = jnp.float32
BF16 = jnp.bfloat16
NN = (((1,), (0,)), ((), ()))
TN = (((0,), (0,)), ((), ()))
NT = (((1,), (1,)), ((), ()))
BLOCK = 128
MESH = pl.DeviceIdType.MESH


def split(x):
    high = x.astype(BF16)
    return high, (x - high.astype(F32)).astype(BF16)


def dot(left, right, dims):
    return lax.dot_general(left, right, dims, preferred_element_type=F32)


def dot3(left, right, dims=NN):
    (lh, ll), (rh, rl) = left, right
    return dot(lh, rh, dims) + (dot(lh, rl, dims) + dot(ll, rh, dims))


def inverse(square, upper):
    size = square.shape[0]
    row = lax.broadcasted_iota(jnp.int32, (size, size), 0)
    col = lax.broadcasted_iota(jnp.int32, (size, size), 1)
    eye = jnp.where(row == col, 1.0, 0.0)
    if upper:
        on_diag = jnp.where(row == col, square, 0.0)
        strict = jnp.where(col > row, square, 0.0) / jnp.sum(on_diag, axis=1, keepdims=True)
    else:
        strict = jnp.where(col < row, square, 0.0)
    result = eye - strict
    halves = split(strict)
    power = dot3(halves, halves)
    reach = 2
    while reach < size:
        halves = split(power)
        result = result + dot3(split(result), halves)
        reach *= 2
        if reach < size:
            power = dot3(halves, halves)
    if upper:
        result = result / jnp.sum(on_diag, axis=0, keepdims=True)
    return result


def prep_kernel(pre, u_ref, l_ref, b_ref, lb_ref, vb_ref, piv_ref, pack_ref, extra_ref, coup_ref, pick_ref):
    i = lax.axis_index("prow")
    j = lax.axis_index("pcol")
    cols = u_ref.shape[1]
    chunk = pick_ref.shape[1]
    mine = pl.ds(pl.multiple_of(j * chunk, chunk), chunk)
    ratio = cols // u_ref.shape[0]
    pack_ref[:, :cols] = jnp.where(i // ratio > j, l_ref[...], u_ref[...])
    pack_ref[:, cols:] = b_ref[:, mine]
    extra_ref[...] = l_ref[...]
    if pre:

        @pl.when(i // ratio == j)
        def _():
            at = pl.multiple_of((i % ratio) * BLOCK, BLOCK)
            pack_ref[:, pl.ds(at, BLOCK)] = inverse(u_ref[:, pl.ds(at, BLOCK)], True)
            extra_ref[:, pl.ds(at, BLOCK)] = inverse(l_ref[:, pl.ds(at, BLOCK)], False)

    coup_ref[...] = dot3(split(vb_ref[...]), split(lb_ref[...]), TN)
    rows = vb_ref.shape[0]
    total = piv_ref.shape[1]
    local = piv_ref[...] - i * rows
    hot = jnp.where(lax.broadcasted_iota(jnp.int32, (rows, total), 0) == local, 1.0, 0.0).astype(BF16)
    part = vb_ref[:, mine]
    first, rest = split(part)
    second = (part - first.astype(F32)).astype(BF16)
    third = (part - first.astype(F32) - second.astype(F32)).astype(BF16)
    pick_ref[...] = dot(hot, first, TN) + dot(hot, second, TN) + dot(hot, third, TN)


def comm_kernel(n, m, m_ref, e_ref, coup_ref, pick_ref, up_ref, gm, ge, gc, gu, xp, cslots, xslots, xparts,
                ring_s, ring_r, side_s, side_r, cross_s, cross_r, sum_s, sum_r, pick_s, pick_r, x_s, x_r, up_s, up_r):
    i = lax.axis_index("prow")
    j = lax.axis_index("pcol")
    half = n // 2
    rows, cols = e_ref.shape
    ratio = cols // rows
    crow = cslots.shape[1]
    odd = i % 2
    pos = odd * (n - 1 - i // 2) + (1 - odd) * (i // 2)

    def member(at):
        at = (at + n) % n
        back = at // half
        return (1 - back) * 2 * at + back * (2 * (n - 1 - at) + 1)

    right, left = member(pos + 1), member(pos - 1)
    across = (j + m // 2) % m
    beside = j + 1 - 2 * (j % 2)
    owners = (j, across)
    guests = (beside, (beside + m // 2) % m)
    parity = j % 2

    barrier = pltpu.get_barrier_semaphore()
    for d in range(1, n):
        pl.semaphore_signal(barrier, inc=1, device_id=((i + d) % n, j), device_id_type=MESH)
    for d in range(1, m):
        pl.semaphore_signal(barrier, inc=1, device_id=(i, (j + d) % m), device_id_type=MESH)
    pl.semaphore_wait(barrier, n + m - 2)

    pending = []

    def guard(cond, action):
        if cond is None:
            action()
        else:
            pl.when(cond)(action)

    def both(one, two):
        if one is None or two is None:
            return two if one is None else one
        return one & two

    def send(src, dst, s_sem, r_sem, to, cond=None):
        copy = pltpu.make_async_remote_copy(src_ref=src, dst_ref=dst, send_sem=s_sem, recv_sem=r_sem, device_id=to, device_id_type=MESH)
        guard(cond, copy.start)
        pending.append((cond, copy))

    def receive(dst, s_sem, r_sem, frm, cond=None):
        copy = pltpu.make_async_remote_copy(src_ref=dst, dst_ref=dst, send_sem=s_sem, recv_sem=r_sem, device_id=frm, device_id_type=MESH)
        guard(cond, copy.wait_recv)

    bufs = (gm, ge, gc)

    def needed(t, row, col):
        return row // ratio == col if t == 1 else None

    def reach(way, hop, par):
        if hop < half:
            return None
        return par == way

    def emit(t, k):
        col = owners[k]
        slot = bufs[t].at[i, col]
        cond = needed(t, i, col)
        for way, to in ((0, right), (1, left)):
            send(slot, slot, ring_s.at[t, k, way, 0], ring_r.at[t, k, way, 0], (to, j), cond)
        send(slot, slot, side_s.at[t, k, 0, 0], side_r.at[t, k, 0, 0], (i, beside), cond)

    def advance(t, k, hop):
        col = owners[k]
        for way, to, frm in ((0, right, left), (1, left, right)):
            row = member(pos - hop) if way == 0 else member(pos + hop)
            slot = bufs[t].at[row, col]
            cond = both(needed(t, row, col), reach(way, hop, parity))
            receive(slot, ring_s.at[t, k, way, hop - 1], ring_r.at[t, k, way, hop - 1], (frm, j), cond)
            if hop < half:
                onward = both(needed(t, row, col), reach(way, hop + 1, parity))
                send(slot, slot, ring_s.at[t, k, way, hop], ring_r.at[t, k, way, hop], (to, j), onward)
            send(slot, slot, side_s.at[t, k, way, hop], side_r.at[t, k, way, hop], (i, beside), cond)

    def side_arrivals(t, k):
        col = guests[k]
        for hop in range(half + 1):
            for way in (0, 1):
                if hop == 0 and way == 1:
                    continue
                row = i if hop == 0 else (member(pos - hop) if way == 0 else member(pos + hop))
                limit = None if hop == 0 else reach(way, hop, 1 - parity)
                receive(bufs[t].at[row, col], side_s.at[t, k, way, hop], side_r.at[t, k, way, hop], (i, beside), both(needed(t, row, col), limit))

    def exchange(t):
        slot = bufs[t].at[i, j]
        send(slot, slot, cross_s.at[t], cross_r.at[t], (i, across), needed(t, i, j))

    def exchanged(t):
        receive(bufs[t].at[i, across], cross_s.at[t], cross_r.at[t], (i, across), needed(t, i, across))

    gm[i, j] = m_ref[...]
    ge[i, j] = e_ref[...]
    exchange(0)
    exchange(1)
    emit(0, 0)
    emit(1, 0)
    for d in range(1, n):
        to = (i + d) % n
        send(coup_ref.at[pl.ds(to * crow, crow)], cslots.at[d - 1], sum_s.at[d - 1], sum_r.at[d - 1], (to, j))
    gu[j] = up_ref[...]
    send(gu.at[j], gu.at[j], up_s.at[0], up_r.at[0], (i, across))
    send(gu.at[j], gu.at[j], up_s.at[1], up_r.at[1], (i, beside))
    exchanged(0)
    exchanged(1)
    emit(0, 1)
    emit(1, 1)
    for t in (0, 1):
        for k in (0, 1):
            advance(t, k, 1)
    total = coup_ref[pl.ds(i * crow, crow), :]
    for d in range(1, n):
        receive(cslots.at[d - 1], sum_s.at[d - 1], sum_r.at[d - 1], ((i - d + n) % n, j))
        total = total + cslots[d - 1]
    gc[i, j] = total
    exchange(2)
    emit(2, 0)
    for t in (0, 1):
        for k in (0, 1):
            advance(t, k, 2)
    exchanged(2)
    emit(2, 1)
    for d in range(1, n):
        to = (i + d) % n
        send(pick_ref.at[pl.ds(to * rows, rows)], xslots.at[d - 1], pick_s.at[d - 1], pick_r.at[d - 1], (to, j))
    for hop in range(3, half + 2):
        for t in (0, 1, 2):
            for k in (0, 1):
                if t == 2:
                    advance(t, k, hop - 2)
                elif hop <= half:
                    advance(t, k, hop)
    for k in (0, 1):
        advance(2, k, half)
    receive(gu.at[across], up_s.at[0], up_r.at[0], (i, across))
    send(gu.at[across], gu.at[across], up_s.at[2], up_r.at[2], (i, beside))
    own = pick_ref[pl.ds(i * rows, rows), :]
    for d in range(1, n):
        receive(xslots.at[d - 1], pick_s.at[d - 1], pick_r.at[d - 1], ((i - d + n) % n, j))
        own = own + xslots[d - 1]
    xparts[j] = own
    for d in range(1, m):
        send(xparts.at[j], xparts.at[j], x_s.at[d - 1], x_r.at[d - 1], (i, (j + d) % m))
    for t in (0, 1, 2):
        for k in (0, 1):
            side_arrivals(t, k)
    receive(gu.at[beside], up_s.at[1], up_r.at[1], (i, beside))
    receive(gu.at[guests[1]], up_s.at[2], up_r.at[2], (i, beside))
    chunk = xparts.shape[2]
    for d in range(1, m):
        frm = (j - d + m) % m
        receive(xparts.at[frm], x_s.at[d - 1], x_r.at[d - 1], (i, frm))
    for q in range(m):
        xp[:, q * chunk : (q + 1) * chunk] = xparts[q]
    for cond, copy in pending:
        guard(cond, copy.wait_send)


def main_kernel(pre, n_row, n_col, g_ref, e_ref, c_ref, up_ref, br_ref, vb_ref, piv_ref, wr_ref, xr_ref, uh, ul, lh, ll, bs, cs, wh, wl):
    i = lax.axis_index("prow")
    rows = g_ref.shape[1]
    cols = up_ref.shape[0] // n_col
    chunk = g_ref.shape[2] - cols
    crow = c_ref.shape[1]
    total = uh.shape[0]
    for a in range(n_row):
        for b in range(n_col):
            at = a * n_col + b
            rs = slice(a * rows, (a + 1) * rows)
            cs_ = slice(b * cols, (b + 1) * cols)
            place = a // (cols // rows)
            if place <= b:
                uh[rs, cs_], ul[rs, cs_] = split(g_ref[at, :, :cols])
            if place == b:
                lh[rs, cs_], ll[rs, cs_] = split(e_ref[at])
            if place > b:
                lh[rs, cs_], ll[rs, cs_] = split(g_ref[at, :, :cols])
            bs[rs, b * chunk : (b + 1) * chunk] = g_ref[at, :, cols:]
            cs[a * crow : (a + 1) * crow, cs_] = c_ref[at]
    count = total // BLOCK
    if not pre:
        for p in range(count):
            sl = slice(p * BLOCK, (p + 1) * BLOCK)
            uh[sl, sl], ul[sl, sl] = split(inverse(uh[sl, sl].astype(F32) + ul[sl, sl].astype(F32), True))
            lh[sl, sl], ll[sl, sl] = split(inverse(lh[sl, sl].astype(F32) + ll[sl, sl].astype(F32), False))
    for p in range(count):
        first = p * BLOCK
        sl = slice(first, first + BLOCK)
        rhs = bs[sl, :].T
        if p:
            rhs = rhs - dot3((wh[:, :first], wl[:, :first]), (uh[:first, sl], ul[:first, sl]))
        out = dot3(split(rhs), (uh[sl, sl], ul[sl, sl]))
        cs[:, sl] = out - cs[:, sl]
        wh[:, sl], wl[:, sl] = split(out)
    tile = 256
    for t in range(up_ref.shape[1] // tile):
        ts = slice(t * tile, (t + 1) * tile)
        update = dot3((wh[...], wl[...]), split(up_ref[:, ts]))
        wr_ref[ts, :] = br_ref[ts, :] - update.T
    for p in reversed(range(count)):
        first = p * BLOCK
        last = first + BLOCK
        sl = slice(first, last)
        rhs = cs[:, sl]
        if last < total:
            rhs = rhs - dot3((wh[:, last:], wl[:, last:]), (lh[last:, sl], ll[last:, sl]))
        out = dot3(split(rhs), (lh[sl, sl], ll[sl, sl]))
        cs[:, sl] = out
        wh[:, sl], wl[:, sl] = split(out)
    all_rows = vb_ref.shape[0]
    for t in range(all_rows // tile):
        ts = slice(t * tile, (t + 1) * tile)
        local = piv_ref[...] - (i * all_rows + t * tile)
        hit = lax.broadcasted_iota(jnp.int32, (tile, total), 0) == local
        hot = jnp.where(hit, 1.0, 0.0)
        used = jnp.sum(hot, axis=1, keepdims=True) > 0.5
        hot = hot.astype(BF16)
        new = dot(hot, wh[...], NT) + dot(hot, wl[...], NT)
        xr_ref[ts, :] = jnp.where(used, new, vb_ref[ts, :])


def body(n_row, n_col, b_panel, b_rest, u_diag, u_panel, l_diag, l_below, v_below, pivot):
    rows, cols = u_diag.shape
    total, rhs = pivot.shape[0], b_panel.shape[1]
    chunk = rhs // n_col
    pre = rows == BLOCK
    piv = pivot[None, :]
    vm = pl.BlockSpec(memory_space=pltpu.VMEM)
    params = pltpu.CompilerParams(vmem_limit_bytes=56 << 20)
    pack, extra, coup, pick = pl.pallas_call(
        functools.partial(prep_kernel, pre),
        out_shape=(
            jax.ShapeDtypeStruct((rows, cols + chunk), F32),
            jax.ShapeDtypeStruct((rows, cols), F32),
            jax.ShapeDtypeStruct((rhs, cols), F32),
            jax.ShapeDtypeStruct((total, chunk), F32),
        ),
        in_specs=[vm] * 6,
        out_specs=(vm,) * 4,
        compiler_params=params,
    )(u_diag, l_diag, b_panel, l_below, v_below, piv)
    if n_row == 8 and n_col == 4:
        crow, half = rhs // n_row, n_row // 2
        dma = pltpu.SemaphoreType.DMA
        gm, ge, gc, gu, x_panel = pl.pallas_call(
            functools.partial(comm_kernel, n_row, n_col),
            out_shape=(
                jax.ShapeDtypeStruct((n_row, n_col, rows, cols + chunk), F32),
                jax.ShapeDtypeStruct((n_row, n_col, rows, cols), F32),
                jax.ShapeDtypeStruct((n_row, n_col, crow, cols), F32),
                jax.ShapeDtypeStruct((n_col,) + u_panel.shape, F32),
                jax.ShapeDtypeStruct((rows, rhs), F32),
            ),
            in_specs=[vm] * 5,
            out_specs=(vm,) * 5,
            scratch_shapes=[
                pltpu.VMEM((n_row - 1, crow, cols), F32),
                pltpu.VMEM((n_row - 1, rows, chunk), F32),
                pltpu.VMEM((n_col, rows, chunk), F32),
                dma((3, 2, 2, half)),
                dma((3, 2, 2, half)),
                dma((3, 2, 2, half + 1)),
                dma((3, 2, 2, half + 1)),
                dma((3,)),
                dma((3,)),
                dma((n_row - 1,)),
                dma((n_row - 1,)),
                dma((n_row - 1,)),
                dma((n_row - 1,)),
                dma((n_col - 1,)),
                dma((n_col - 1,)),
                dma((3,)),
                dma((3,)),
            ],
            compiler_params=pltpu.CompilerParams(vmem_limit_bytes=56 << 20, collective_id=0, has_side_effects=True),
        )(pack, extra, coup, pick, u_panel)
        gathered = gm.reshape(n_row * n_col, rows, cols + chunk)
        extras = ge.reshape(n_row * n_col, rows, cols)
        call = gc.reshape(n_row * n_col, crow, cols)
        upan = gu.reshape(n_col * u_panel.shape[0], u_panel.shape[1])
    else:
        gathered = lax.all_gather(pack, ("prow", "pcol"), axis=0)
        extras = lax.all_gather(extra, ("prow", "pcol"), axis=0)
        upan = lax.all_gather(u_panel, "pcol", axis=0, tiled=True)
        csum = lax.psum_scatter(coup, "prow", scatter_dimension=0, tiled=True)
        call = lax.all_gather(csum, ("prow", "pcol"), axis=0)
        xsum = lax.psum_scatter(pick, "prow", scatter_dimension=0, tiled=True)
        x_panel = lax.all_gather(xsum, "pcol", axis=1, tiled=True)
    w_rest, x_rest = pl.pallas_call(
        functools.partial(main_kernel, pre, n_row, n_col),
        out_shape=(jax.ShapeDtypeStruct(b_rest.shape, F32), jax.ShapeDtypeStruct(v_below.shape, F32)),
        in_specs=[vm] * 7,
        out_specs=(vm, vm),
        scratch_shapes=[pltpu.VMEM((total, total), BF16)] * 4
        + [pltpu.VMEM((total, rhs), F32), pltpu.VMEM((rhs, total), F32)]
        + [pltpu.VMEM((rhs, total), BF16)] * 2,
        compiler_params=params,
    )(gathered, extras, call, upan, b_rest, v_below, piv)
    return w_rest, x_panel, x_rest


def solution(mesh):
    in_specs = (
        P("prow", None),
        P("prow", None),
        P("prow", "pcol"),
        P("pcol", "prow"),
        P("prow", "pcol"),
        P("prow", "pcol"),
        P("prow", None),
        P(),
    )
    out_specs = (P("prow", None), P("prow", None), P("prow", None))
    step = functools.partial(body, mesh.shape["prow"], mesh.shape["pcol"])
    return jax.shard_map(step, mesh=mesh, in_specs=in_specs, out_specs=out_specs, check_vma=False)
```

```python
import functools

import jax
import jax.numpy as jnp
from jax import lax
from jax.experimental import pallas as pl
from jax.experimental.pallas import tpu as pltpu
from jax.sharding import PartitionSpec as P

F32 = jnp.float32
BF16 = jnp.bfloat16
NN = (((1,), (0,)), ((), ()))
TN = (((0,), (0,)), ((), ()))
NT = (((1,), (1,)), ((), ()))
BLOCK = 128
MESH = pl.DeviceIdType.MESH


def split(x):
    high = x.astype(BF16)
    return high, (x - high.astype(F32)).astype(BF16)


def dot(left, right, dims):
    return lax.dot_general(left, right, dims, preferred_element_type=F32)


def dot3(left, right, dims=NN):
    (lh, ll), (rh, rl) = left, right
    return dot(lh, rh, dims) + (dot(lh, rl, dims) + dot(ll, rh, dims))


def inverse(square, upper):
    size = square.shape[0]
    row = lax.broadcasted_iota(jnp.int32, (size, size), 0)
    col = lax.broadcasted_iota(jnp.int32, (size, size), 1)
    eye = jnp.where(row == col, 1.0, 0.0)
    if upper:
        on_diag = jnp.where(row == col, square, 0.0)
        strict = jnp.where(col > row, square, 0.0) / jnp.sum(on_diag, axis=1, keepdims=True)
    else:
        strict = jnp.where(col < row, square, 0.0)
    result = eye - strict
    halves = split(strict)
    power = dot3(halves, halves)
    reach = 2
    while reach < size:
        halves = split(power)
        result = result + dot3(split(result), halves)
        reach *= 2
        if reach < size:
            power = dot3(halves, halves)
    if upper:
        result = result / jnp.sum(on_diag, axis=0, keepdims=True)
    return result


def prep_kernel(pre, u_ref, l_ref, b_ref, lb_ref, vb_ref, piv_ref, pack_ref, extra_ref, coup_ref, pick_ref):
    i = lax.axis_index("prow")
    j = lax.axis_index("pcol")
    cols = u_ref.shape[1]
    chunk = pick_ref.shape[1]
    mine = pl.ds(pl.multiple_of(j * chunk, chunk), chunk)
    ratio = cols // u_ref.shape[0]
    pack_ref[:, :cols] = jnp.where(i // ratio > j, l_ref[...], u_ref[...])
    pack_ref[:, cols:] = b_ref[:, mine]
    extra_ref[...] = l_ref[...]
    if pre:

        @pl.when(i // ratio == j)
        def _():
            at = pl.multiple_of((i % ratio) * BLOCK, BLOCK)
            pack_ref[:, pl.ds(at, BLOCK)] = inverse(u_ref[:, pl.ds(at, BLOCK)], True)
            extra_ref[:, pl.ds(at, BLOCK)] = inverse(l_ref[:, pl.ds(at, BLOCK)], False)

    coup_ref[...] = dot3(split(vb_ref[...]), split(lb_ref[...]), TN)
    pick_rows(i, vb_ref, piv_ref, pick_ref, mine)


def pick_rows(i, vb_ref, piv_ref, pick_ref, mine):
    rows = vb_ref.shape[0]
    total = piv_ref.shape[1]
    local = piv_ref[...] - i * rows
    hot = jnp.where(lax.broadcasted_iota(jnp.int32, (rows, total), 0) == local, 1.0, 0.0).astype(BF16)
    part = vb_ref[:, mine]
    first, _ = split(part)
    second = (part - first.astype(F32)).astype(BF16)
    third = (part - first.astype(F32) - second.astype(F32)).astype(BF16)
    pick_ref[...] = dot(hot, first, TN) + dot(hot, second, TN) + dot(hot, third, TN)


def assemble(n_row, n_col, g_ref, e_ref, uh, ul, lh, ll, bs):
    rows, cols = e_ref.shape[2:]
    chunk = g_ref.shape[3] - cols
    for a in range(n_row):
        for b in range(n_col):
            rs = slice(a * rows, (a + 1) * rows)
            cs_ = slice(b * cols, (b + 1) * cols)
            place = a // (cols // rows)
            if place <= b:
                uh[rs, cs_], ul[rs, cs_] = split(g_ref[a, b, :, :cols])
            if place == b:
                lh[rs, cs_], ll[rs, cs_] = split(e_ref[a, b])
            if place > b:
                lh[rs, cs_], ll[rs, cs_] = split(g_ref[a, b, :, :cols])
            bs[rs, b * chunk : (b + 1) * chunk] = g_ref[a, b, :, cols:]


def first_solve(bs, cs, wh, wl, uh, ul, service):
    for p in range(bs.shape[0] // BLOCK):
        first = p * BLOCK
        sl = slice(first, first + BLOCK)
        rhs = bs[sl, :].T
        if p:
            rhs = rhs - dot3((wh[:, :first], wl[:, :first]), (uh[:first, sl], ul[:first, sl]))
        out = dot3(split(rhs), (uh[sl, sl], ul[sl, sl]))
        cs[:, sl] = out
        wh[:, sl], wl[:, sl] = split(out)
        service(p)


def rest_update(wh, wl, columns, br_ref, wr_ref):
    tile = 256
    for t in range(wr_ref.shape[0] // tile):
        ts = slice(t * tile, (t + 1) * tile)
        wr_ref[ts, :] = br_ref[ts, :] - dot3((wh[...], wl[...]), split(columns(ts))).T


def second_solve(cs, wh, wl, lh, ll):
    total = cs.shape[1]
    for p in reversed(range(total // BLOCK)):
        last = (p + 1) * BLOCK
        sl = slice(p * BLOCK, last)
        rhs = cs[:, sl]
        if last < total:
            rhs = rhs - dot3((wh[:, last:], wl[:, last:]), (lh[last:, sl], ll[last:, sl]))
        wh[:, sl], wl[:, sl] = split(dot3(split(rhs), (lh[sl, sl], ll[sl, sl])))


def interchange(i, wh, wl, vb_ref, piv_ref, xr_ref):
    tile = 256
    all_rows, total = vb_ref.shape[0], piv_ref.shape[1]
    for t in range(all_rows // tile):
        ts = slice(t * tile, (t + 1) * tile)
        local = piv_ref[...] - (i * all_rows + t * tile)
        hot = jnp.where(lax.broadcasted_iota(jnp.int32, (tile, total), 0) == local, 1.0, 0.0)
        used = jnp.sum(hot, axis=1, keepdims=True) > 0.5
        hot = hot.astype(BF16)
        new = dot(hot, wh[...], NT) + dot(hot, wl[...], NT)
        xr_ref[ts, :] = jnp.where(used, new, vb_ref[ts, :])


def whole_kernel(n, m, u_ref, l_ref, b_ref, lb_ref, vb_ref, piv_ref, up_ref, br_ref, wr_ref, xr_ref, xp,
                 gm, ge, gc, gu, coup_ref, pick_ref, uh, ul, lh, ll, bs, cs, wh, wl, cslots, xslots, xparts,
                 ring_s, ring_r, side_s, side_r, cross_s, cross_r, sum_s, sum_r, pick_s, pick_r, x_s, x_r, up_s, up_r, late_s, late_r):
    i = lax.axis_index("prow")
    j = lax.axis_index("pcol")
    half = n // 2
    rows, cols = u_ref.shape
    ratio = cols // rows
    crow = cslots.shape[1]
    odd = i % 2
    pos = odd * (n - 1 - i // 2) + (1 - odd) * (i // 2)

    def member(at):
        at = (at + n) % n
        back = at // half
        return (1 - back) * 2 * at + back * (2 * (n - 1 - at) + 1)

    right, left = member(pos + 1), member(pos - 1)
    across = (j + m // 2) % m
    beside = j + 1 - 2 * (j % 2)
    owners = (j, across)
    guests = (beside, (beside + m // 2) % m)
    parity = j % 2

    barrier = pltpu.get_barrier_semaphore()
    for d in range(1, n):
        pl.semaphore_signal(barrier, inc=1, device_id=((i + d) % n, j), device_id_type=MESH)
    for d in range(1, m):
        pl.semaphore_signal(barrier, inc=1, device_id=(i, (j + d) % m), device_id_type=MESH)

    pending = []

    def guard(cond, action):
        if cond is None:
            action()
        else:
            pl.when(cond)(action)

    def both(one, two):
        if one is None or two is None:
            return two if one is None else one
        return one & two

    def send(src, dst, s_sem, r_sem, to, cond=None):
        copy = pltpu.make_async_remote_copy(src_ref=src, dst_ref=dst, send_sem=s_sem, recv_sem=r_sem, device_id=to, device_id_type=MESH)
        guard(cond, copy.start)
        pending.append((cond, copy))

    def receive(dst, s_sem, r_sem, frm, cond=None):
        copy = pltpu.make_async_remote_copy(src_ref=dst, dst_ref=dst, send_sem=s_sem, recv_sem=r_sem, device_id=frm, device_id_type=MESH)
        guard(cond, copy.wait_recv)

    bufs = (gm, ge, gc)

    def needed(t, row, col):
        return row // ratio == col if t == 1 else None

    def reach(way, hop, par):
        if hop < half:
            return None
        return par == way

    def emit(t, k):
        col = owners[k]
        slot = bufs[t].at[i, col]
        cond = needed(t, i, col)
        for way, to in ((0, right), (1, left)):
            send(slot, slot, ring_s.at[t, k, way, 0], ring_r.at[t, k, way, 0], (to, j), cond)
        send(slot, slot, side_s.at[t, k, 0, 0], side_r.at[t, k, 0, 0], (i, beside), cond)
        if t == 2:
            send(slot, slot, late_s.at[0, 0], late_r.at[0, 0], (i, across))

    def crossed(hop):
        for way in (0, 1) if hop else (0,):
            row = member(pos - hop) if way == 0 else member(pos + hop)
            slot = gc.at[row, across]
            cond = reach(way, hop, parity)
            receive(slot, late_s.at[way, hop], late_r.at[way, hop], (i, across), cond)
            send(slot, slot, side_s.at[2, 1, way, hop], side_r.at[2, 1, way, hop], (i, beside), cond)

    def advance(t, k, hop):
        col = owners[k]
        for way, to, frm in ((0, right, left), (1, left, right)):
            row = member(pos - hop) if way == 0 else member(pos + hop)
            slot = bufs[t].at[row, col]
            cond = both(needed(t, row, col), reach(way, hop, parity))
            receive(slot, ring_s.at[t, k, way, hop - 1], ring_r.at[t, k, way, hop - 1], (frm, j), cond)
            if hop < half:
                onward = both(needed(t, row, col), reach(way, hop + 1, parity))
                send(slot, slot, ring_s.at[t, k, way, hop], ring_r.at[t, k, way, hop], (to, j), onward)
            if t == 2:
                send(slot, slot, late_s.at[way, hop], late_r.at[way, hop], (i, across), cond)
            send(slot, slot, side_s.at[t, k, way, hop], side_r.at[t, k, way, hop], (i, beside), cond)

    def side_arrivals(t, k):
        col = guests[k]
        for hop in range(half + 1):
            for way in (0, 1):
                if hop == 0 and way == 1:
                    continue
                row = i if hop == 0 else (member(pos - hop) if way == 0 else member(pos + hop))
                limit = None if hop == 0 else reach(way, hop, 1 - parity)
                receive(bufs[t].at[row, col], side_s.at[t, k, way, hop], side_r.at[t, k, way, hop], (i, beside), both(needed(t, row, col), limit))

    def exchange(t):
        slot = bufs[t].at[i, j]
        send(slot, slot, cross_s.at[t], cross_r.at[t], (i, across), needed(t, i, j))

    def exchanged(t):
        receive(bufs[t].at[i, across], cross_s.at[t], cross_r.at[t], (i, across), needed(t, i, across))

    chunk = pick_ref.shape[1]
    mine = pl.ds(pl.multiple_of(j * chunk, chunk), chunk)
    own = gm.at[i, j]
    more = ge.at[i, j]
    own[:, :cols] = jnp.where(i // ratio > j, l_ref[...], u_ref[...])
    own[:, cols:] = b_ref[:, mine]

    @pl.when(i // ratio == j)
    def _():
        at = pl.multiple_of((i % ratio) * BLOCK, BLOCK)
        more[...] = l_ref[...]
        own[:, pl.ds(at, BLOCK)] = inverse(u_ref[:, pl.ds(at, BLOCK)], True)
        more[:, pl.ds(at, BLOCK)] = inverse(l_ref[:, pl.ds(at, BLOCK)], False)

    pl.semaphore_wait(barrier, n + m - 2)
    exchange(0)
    exchange(1)
    emit(0, 0)
    emit(1, 0)
    coup_ref[...] = dot3(split(vb_ref[...]), split(lb_ref[...]), TN)
    for d in range(1, n):
        to = (i + d) % n
        send(coup_ref.at[pl.ds(to * crow, crow)], cslots.at[d - 1], sum_s.at[d - 1], sum_r.at[d - 1], (to, j))
    exchanged(0)
    exchanged(1)
    emit(0, 1)
    emit(1, 1)
    gu[j] = up_ref[...]
    send(gu.at[j], gu.at[j], up_s.at[0], up_r.at[0], (i, across))
    send(gu.at[j], gu.at[j], up_s.at[1], up_r.at[1], (i, beside))
    for t in (0, 1):
        for k in (0, 1):
            advance(t, k, 1)
    pick_rows(i, vb_ref, piv_ref, pick_ref, mine)
    for t in (0, 1):
        for k in (0, 1):
            advance(t, k, 2)
    total = coup_ref[pl.ds(i * crow, crow), :]
    for d in range(1, n):
        receive(cslots.at[d - 1], sum_s.at[d - 1], sum_r.at[d - 1], ((i - d + n) % n, j))
        total = total + cslots[d - 1]
    gc[i, j] = total
    emit(2, 0)
    for t in (0, 1):
        for k in (0, 1):
            advance(t, k, 3)
    advance(2, 0, 1)
    for d in range(1, n):
        to = (i + d) % n
        send(pick_ref.at[pl.ds(to * rows, rows)], xslots.at[d - 1], pick_s.at[d - 1], pick_r.at[d - 1], (to, j))
    for t in (0, 1):
        for k in (0, 1):
            advance(t, k, half)
    advance(2, 0, 2)
    crossed(0)
    for t in (0, 1):
        for k in (0, 1):
            side_arrivals(t, k)
    assemble(n, m, gm, ge, uh, ul, lh, ll, bs)
    advance(2, 0, 3)
    crossed(1)
    receive(gu.at[across], up_s.at[0], up_r.at[0], (i, across))
    send(gu.at[across], gu.at[across], up_s.at[2], up_r.at[2], (i, beside))

    def service(p):
        if p == 1:
            advance(2, 0, half)
        if p in (2, 4, 6):
            crossed(p // 2 + 1)

    first_solve(bs, cs, wh, wl, uh, ul, service)
    own = pick_ref[pl.ds(i * rows, rows), :]
    for d in range(1, n):
        receive(xslots.at[d - 1], pick_s.at[d - 1], pick_r.at[d - 1], ((i - d + n) % n, j))
        own = own + xslots[d - 1]
    xparts[j] = own
    for d in range(1, m):
        send(xparts.at[j], xparts.at[j], x_s.at[d - 1], x_r.at[d - 1], (i, (j + d) % m))
    receive(gu.at[beside], up_s.at[1], up_r.at[1], (i, beside))
    receive(gu.at[guests[1]], up_s.at[2], up_r.at[2], (i, beside))
    rest_update(wh, wl, lambda ts: jnp.concatenate([gu[q, :, ts] for q in range(m)], axis=0), br_ref, wr_ref)
    for k in (0, 1):
        side_arrivals(2, k)
    for a in range(n):
        for b in range(m):
            cs[a * crow : (a + 1) * crow, b * cols : (b + 1) * cols] -= gc[a, b]
    second_solve(cs, wh, wl, lh, ll)
    interchange(i, wh, wl, vb_ref, piv_ref, xr_ref)
    for d in range(1, m):
        frm = (j - d + m) % m
        receive(xparts.at[frm], x_s.at[d - 1], x_r.at[d - 1], (i, frm))
    for q in range(m):
        xp[:, q * chunk : (q + 1) * chunk] = xparts[q]
    for cond, copy in pending:
        guard(cond, copy.wait_send)


def main_kernel(pre, g_ref, e_ref, c_ref, up_ref, br_ref, vb_ref, piv_ref, wr_ref, xr_ref, uh, ul, lh, ll, bs, cs, wh, wl):
    n_row, n_col, crow, cols = c_ref.shape
    assemble(n_row, n_col, g_ref, e_ref, uh, ul, lh, ll, bs)
    if not pre:
        for p in range(uh.shape[0] // BLOCK):
            sl = slice(p * BLOCK, (p + 1) * BLOCK)
            uh[sl, sl], ul[sl, sl] = split(inverse(uh[sl, sl].astype(F32) + ul[sl, sl].astype(F32), True))
            lh[sl, sl], ll[sl, sl] = split(inverse(lh[sl, sl].astype(F32) + ll[sl, sl].astype(F32), False))
    first_solve(bs, cs, wh, wl, uh, ul, lambda p: None)
    for a in range(n_row):
        for b in range(n_col):
            cs[a * crow : (a + 1) * crow, b * cols : (b + 1) * cols] -= c_ref[a, b]
    rest_update(wh, wl, lambda ts: up_ref[:, ts], br_ref, wr_ref)
    second_solve(cs, wh, wl, lh, ll)
    interchange(lax.axis_index("prow"), wh, wl, vb_ref, piv_ref, xr_ref)


def body(n_row, n_col, b_panel, b_rest, u_diag, u_panel, l_diag, l_below, v_below, pivot):
    rows, cols = u_diag.shape
    total, rhs = pivot.shape[0], b_panel.shape[1]
    chunk = rhs // n_col
    pre = rows == BLOCK
    piv = pivot[None, :]
    vm = pl.BlockSpec(memory_space=pltpu.VMEM)
    params = pltpu.CompilerParams(vmem_limit_bytes=56 << 20)
    halves = [pltpu.VMEM((total, total), BF16)] * 4
    halves += [pltpu.VMEM((total, rhs), F32), pltpu.VMEM((rhs, total), F32)]
    halves += [pltpu.VMEM((rhs, total), BF16)] * 2
    if pre and n_row == 8 and n_col == 4:
        crow, half = rhs // n_row, n_row // 2
        shapes = [(3, 2, 2, half), (3, 2, 2, half + 1), (2,), (n_row - 1,), (n_row - 1,), (n_col - 1,), (3,), (2, half + 1)]
        w_rest, x_rest, x_panel = pl.pallas_call(
            functools.partial(whole_kernel, n_row, n_col),
            out_shape=(
                jax.ShapeDtypeStruct(b_rest.shape, F32),
                jax.ShapeDtypeStruct(v_below.shape, F32),
                jax.ShapeDtypeStruct((rows, rhs), F32),
            ),
            in_specs=[vm] * 8,
            out_specs=(vm,) * 3,
            scratch_shapes=[
                pltpu.VMEM((n_row, n_col, rows, cols + chunk), F32),
                pltpu.VMEM((n_row, n_col, rows, cols), F32),
                pltpu.VMEM((n_row, n_col, crow, cols), F32),
                pltpu.VMEM((n_col,) + u_panel.shape, F32),
                pltpu.VMEM((rhs, cols), F32),
                pltpu.VMEM((total, chunk), F32),
            ]
            + halves
            + [
                pltpu.VMEM((n_row - 1, crow, cols), F32),
                pltpu.VMEM((n_row - 1, rows, chunk), F32),
                pltpu.VMEM((n_col, rows, chunk), F32),
            ]
            + [pltpu.SemaphoreType.DMA(shape) for shape in shapes for _ in range(2)],
            compiler_params=pltpu.CompilerParams(vmem_limit_bytes=60 << 20, collective_id=0, has_side_effects=True),
        )(u_diag, l_diag, b_panel, l_below, v_below, piv, u_panel, b_rest)
        return w_rest, x_panel, x_rest
    pack, extra, coup, pick = pl.pallas_call(
        functools.partial(prep_kernel, pre),
        out_shape=(
            jax.ShapeDtypeStruct((rows, cols + chunk), F32),
            jax.ShapeDtypeStruct((rows, cols), F32),
            jax.ShapeDtypeStruct((rhs, cols), F32),
            jax.ShapeDtypeStruct((total, chunk), F32),
        ),
        in_specs=[vm] * 6,
        out_specs=(vm,) * 4,
        compiler_params=params,
    )(u_diag, l_diag, b_panel, l_below, v_below, piv)

    def everywhere(piece):
        return lax.all_gather(piece, ("prow", "pcol"), axis=0).reshape((n_row, n_col) + piece.shape)

    upan = lax.all_gather(u_panel, "pcol", axis=0, tiled=True)
    csum = lax.psum_scatter(coup, "prow", scatter_dimension=0, tiled=True)
    xsum = lax.psum_scatter(pick, "prow", scatter_dimension=0, tiled=True)
    x_panel = lax.all_gather(xsum, "pcol", axis=1, tiled=True)
    w_rest, x_rest = pl.pallas_call(
        functools.partial(main_kernel, pre),
        out_shape=(jax.ShapeDtypeStruct(b_rest.shape, F32), jax.ShapeDtypeStruct(v_below.shape, F32)),
        in_specs=[vm] * 7,
        out_specs=(vm, vm),
        scratch_shapes=halves,
        compiler_params=params,
    )(everywhere(pack), everywhere(extra), everywhere(csum), upan, b_rest, v_below, piv)
    return w_rest, x_panel, x_rest


def solution(mesh):
    in_specs = (
        P("prow", None),
        P("prow", None),
        P("prow", "pcol"),
        P("pcol", "prow"),
        P("prow", "pcol"),
        P("prow", "pcol"),
        P("prow", None),
        P(),
    )
    out_specs = (P("prow", None), P("prow", None), P("prow", None))
    step = functools.partial(body, mesh.shape["prow"], mesh.shape["pcol"])
    return jax.shard_map(step, mesh=mesh, in_specs=in_specs, out_specs=out_specs, check_vma=False)
```

```python
import functools

import jax
import jax.numpy as jnp
from jax import lax
from jax.experimental import pallas as pl
from jax.experimental.pallas import tpu as pltpu
from jax.sharding import PartitionSpec as P

F32 = jnp.float32
BF16 = jnp.bfloat16
NN = (((1,), (0,)), ((), ()))
TN = (((0,), (0,)), ((), ()))
NT = (((1,), (1,)), ((), ()))
BLOCK = 128
MESH = pl.DeviceIdType.MESH


def split(x):
    high = x.astype(BF16)
    return high, (x - high.astype(F32)).astype(BF16)


def dot(left, right, dims):
    return lax.dot_general(left, right, dims, preferred_element_type=F32)


def dot3(left, right, dims=NN):
    (lh, ll), (rh, rl) = left, right
    return dot(lh, rh, dims) + (dot(lh, rl, dims) + dot(ll, rh, dims))


def inverse(square, upper):
    size = square.shape[0]
    row = lax.broadcasted_iota(jnp.int32, (size, size), 0)
    col = lax.broadcasted_iota(jnp.int32, (size, size), 1)
    eye = jnp.where(row == col, 1.0, 0.0)
    if upper:
        on_diag = jnp.where(row == col, square, 0.0)
        strict = jnp.where(col > row, square, 0.0) / jnp.sum(on_diag, axis=1, keepdims=True)
    else:
        strict = jnp.where(col < row, square, 0.0)
    result = eye - strict
    halves = split(strict)
    power = dot3(halves, halves)
    reach = 2
    while reach < size:
        halves = split(power)
        result = result + dot3(split(result), halves)
        reach *= 2
        if reach < size:
            power = dot3(halves, halves)
    if upper:
        result = result / jnp.sum(on_diag, axis=0, keepdims=True)
    return result


def prep_kernel(pre, u_ref, l_ref, b_ref, lb_ref, vb_ref, piv_ref, pack_ref, extra_ref, coup_ref, pick_ref):
    i = lax.axis_index("prow")
    j = lax.axis_index("pcol")
    cols = u_ref.shape[1]
    chunk = pick_ref.shape[1]
    mine = pl.ds(pl.multiple_of(j * chunk, chunk), chunk)
    ratio = cols // u_ref.shape[0]
    pack_ref[:, :cols] = jnp.where(i // ratio > j, l_ref[...], u_ref[...])
    pack_ref[:, cols:] = b_ref[:, mine]
    extra_ref[...] = l_ref[...]
    if pre:

        @pl.when(i // ratio == j)
        def _():
            at = pl.multiple_of((i % ratio) * BLOCK, BLOCK)
            pack_ref[:, pl.ds(at, BLOCK)] = inverse(u_ref[:, pl.ds(at, BLOCK)], True)
            extra_ref[:, pl.ds(at, BLOCK)] = inverse(l_ref[:, pl.ds(at, BLOCK)], False)

    coup_ref[...] = dot3(split(vb_ref[...]), split(lb_ref[...]), TN)
    pick_rows(i, vb_ref, piv_ref, pick_ref, mine)


def pick_rows(i, vb_ref, piv_ref, pick_ref, mine):
    rows = vb_ref.shape[0]
    total = piv_ref.shape[1]
    local = piv_ref[...] - i * rows
    hot = jnp.where(lax.broadcasted_iota(jnp.int32, (rows, total), 0) == local, 1.0, 0.0).astype(BF16)
    part = vb_ref[:, mine]
    first, _ = split(part)
    second = (part - first.astype(F32)).astype(BF16)
    third = (part - first.astype(F32) - second.astype(F32)).astype(BF16)
    pick_ref[...] = dot(hot, first, TN) + dot(hot, second, TN) + dot(hot, third, TN)


def assemble(n_row, n_col, g_ref, e_ref, uh, ul, lh, ll, bs):
    rows, cols = e_ref.shape[2:]
    chunk = g_ref.shape[3] - cols
    for a in range(n_row):
        for b in range(n_col):
            rs = slice(a * rows, (a + 1) * rows)
            cs_ = slice(b * cols, (b + 1) * cols)
            place = a // (cols // rows)
            if place <= b:
                uh[rs, cs_], ul[rs, cs_] = split(g_ref[a, b, :, :cols])
            if place == b:
                lh[rs, cs_], ll[rs, cs_] = split(e_ref[a, b])
            if place > b:
                lh[rs, cs_], ll[rs, cs_] = split(g_ref[a, b, :, :cols])
            bs[rs, b * chunk : (b + 1) * chunk] = g_ref[a, b, :, cols:]


def first_solve(bs, cs, wh, wl, uh, ul, service):
    for p in range(bs.shape[0] // BLOCK):
        first = p * BLOCK
        sl = slice(first, first + BLOCK)
        rhs = bs[sl, :].T
        if p:
            rhs = rhs - dot3((wh[:, :first], wl[:, :first]), (uh[:first, sl], ul[:first, sl]))
        out = dot3(split(rhs), (uh[sl, sl], ul[sl, sl]))
        cs[:, sl] = out
        wh[:, sl], wl[:, sl] = split(out)
        service(p)


def rest_update(wh, wl, columns, br_ref, wr_ref):
    tile = 256
    for t in range(wr_ref.shape[0] // tile):
        ts = slice(t * tile, (t + 1) * tile)
        wr_ref[ts, :] = br_ref[ts, :] - dot3((wh[...], wl[...]), split(columns(ts))).T


def second_solve(cs, wh, wl, lh, ll):
    total = cs.shape[1]
    for p in reversed(range(total // BLOCK)):
        last = (p + 1) * BLOCK
        sl = slice(p * BLOCK, last)
        rhs = cs[:, sl]
        if last < total:
            rhs = rhs - dot3((wh[:, last:], wl[:, last:]), (lh[last:, sl], ll[last:, sl]))
        wh[:, sl], wl[:, sl] = split(dot3(split(rhs), (lh[sl, sl], ll[sl, sl])))


def interchange(i, wh, wl, vb_ref, piv_ref, xr_ref):
    tile = 256
    all_rows, total = vb_ref.shape[0], piv_ref.shape[1]
    for t in range(all_rows // tile):
        ts = slice(t * tile, (t + 1) * tile)
        local = piv_ref[...] - (i * all_rows + t * tile)
        hot = jnp.where(lax.broadcasted_iota(jnp.int32, (tile, total), 0) == local, 1.0, 0.0)
        used = jnp.sum(hot, axis=1, keepdims=True) > 0.5
        hot = hot.astype(BF16)
        new = dot(hot, wh[...], NT) + dot(hot, wl[...], NT)
        xr_ref[ts, :] = jnp.where(used, new, vb_ref[ts, :])


def whole_kernel(n, m, u_ref, l_ref, b_ref, lb_ref, vb_ref, piv_ref, up_ref, br_ref, wr_ref, xr_ref, xp,
                 gm, ge, gc, gu, coup_ref, pick_ref, uh, ul, lh, ll, bs, cs, wh, wl, cslots, xslots, xparts,
                 ring_s, ring_r, side_s, side_r, cross_s, cross_r, sum_s, sum_r, pick_s, pick_r, x_s, x_r, up_s, up_r, late_s, late_r):
    i = lax.axis_index("prow")
    j = lax.axis_index("pcol")
    half = n // 2
    rows, cols = u_ref.shape
    ratio = cols // rows
    crow = cslots.shape[1]
    odd = i % 2
    pos = odd * (n - 1 - i // 2) + (1 - odd) * (i // 2)

    def member(at):
        at = (at + n) % n
        back = at // half
        return (1 - back) * 2 * at + back * (2 * (n - 1 - at) + 1)

    right, left = member(pos + 1), member(pos - 1)
    across = (j + m // 2) % m
    beside = j + 1 - 2 * (j % 2)
    owners = (j, across)
    guests = (beside, (beside + m // 2) % m)
    parity = j % 2

    barrier = pltpu.get_barrier_semaphore()
    for d in range(1, n):
        pl.semaphore_signal(barrier, inc=1, device_id=((i + d) % n, j), device_id_type=MESH)
    for d in range(1, m):
        pl.semaphore_signal(barrier, inc=1, device_id=(i, (j + d) % m), device_id_type=MESH)

    pending = []

    def guard(cond, action):
        if cond is None:
            action()
        else:
            pl.when(cond)(action)

    def both(one, two):
        if one is None or two is None:
            return two if one is None else one
        return one & two

    def send(src, dst, s_sem, r_sem, to, cond=None):
        copy = pltpu.make_async_remote_copy(src_ref=src, dst_ref=dst, send_sem=s_sem, recv_sem=r_sem, device_id=to, device_id_type=MESH)
        guard(cond, copy.start)
        pending.append((cond, copy))

    def receive(dst, s_sem, r_sem, frm, cond=None):
        copy = pltpu.make_async_remote_copy(src_ref=dst, dst_ref=dst, send_sem=s_sem, recv_sem=r_sem, device_id=frm, device_id_type=MESH)
        guard(cond, copy.wait_recv)

    bufs = (gm, ge, gc)

    def needed(t, row, col):
        return row // ratio == col if t == 1 else None

    def reach(way, hop, par):
        if hop < half:
            return None
        return par == way

    def emit(t, k):
        col = owners[k]
        slot = bufs[t].at[i, col]
        cond = needed(t, i, col)
        for way, to in ((0, right), (1, left)):
            send(slot, slot, ring_s.at[t, k, way, 0], ring_r.at[t, k, way, 0], (to, j), cond)
        send(slot, slot, side_s.at[t, k, 0, 0], side_r.at[t, k, 0, 0], (i, beside), cond)
        if t == 2:
            send(slot, slot, late_s.at[0, 0], late_r.at[0, 0], (i, across))

    def crossed(hop):
        for way in (0, 1) if hop else (0,):
            row = member(pos - hop) if way == 0 else member(pos + hop)
            slot = gc.at[row, across]
            cond = reach(way, hop, parity)
            receive(slot, late_s.at[way, hop], late_r.at[way, hop], (i, across), cond)
            send(slot, slot, side_s.at[2, 1, way, hop], side_r.at[2, 1, way, hop], (i, beside), cond)

    def advance(t, k, hop):
        col = owners[k]
        for way, to, frm in ((0, right, left), (1, left, right)):
            row = member(pos - hop) if way == 0 else member(pos + hop)
            slot = bufs[t].at[row, col]
            cond = both(needed(t, row, col), reach(way, hop, parity))
            receive(slot, ring_s.at[t, k, way, hop - 1], ring_r.at[t, k, way, hop - 1], (frm, j), cond)
            if hop < half:
                onward = both(needed(t, row, col), reach(way, hop + 1, parity))
                send(slot, slot, ring_s.at[t, k, way, hop], ring_r.at[t, k, way, hop], (to, j), onward)
            if t == 2:
                send(slot, slot, late_s.at[way, hop], late_r.at[way, hop], (i, across), cond)
            send(slot, slot, side_s.at[t, k, way, hop], side_r.at[t, k, way, hop], (i, beside), cond)

    def side_arrivals(t, k):
        col = guests[k]
        for hop in range(half + 1):
            for way in (0, 1):
                if hop == 0 and way == 1:
                    continue
                row = i if hop == 0 else (member(pos - hop) if way == 0 else member(pos + hop))
                limit = None if hop == 0 else reach(way, hop, 1 - parity)
                receive(bufs[t].at[row, col], side_s.at[t, k, way, hop], side_r.at[t, k, way, hop], (i, beside), both(needed(t, row, col), limit))

    def exchange(t):
        slot = bufs[t].at[i, j]
        send(slot, slot, cross_s.at[t], cross_r.at[t], (i, across), needed(t, i, j))

    def exchanged(t):
        receive(bufs[t].at[i, across], cross_s.at[t], cross_r.at[t], (i, across), needed(t, i, across))

    chunk = pick_ref.shape[1]
    mine = pl.ds(pl.multiple_of(j * chunk, chunk), chunk)
    own = gm.at[i, j]
    more = ge.at[i, j]
    own[:, :cols] = jnp.where(i // ratio > j, l_ref[...], u_ref[...])
    own[:, cols:] = b_ref[:, mine]

    @pl.when(i // ratio == j)
    def _():
        at = pl.multiple_of((i % ratio) * BLOCK, BLOCK)
        more[...] = l_ref[...]
        own[:, pl.ds(at, BLOCK)] = inverse(u_ref[:, pl.ds(at, BLOCK)], True)
        more[:, pl.ds(at, BLOCK)] = inverse(l_ref[:, pl.ds(at, BLOCK)], False)

    pl.semaphore_wait(barrier, n + m - 2)
    exchange(0)
    exchange(1)
    emit(0, 0)
    emit(1, 0)
    coup_ref[...] = dot3(split(vb_ref[...]), split(lb_ref[...]), TN)
    for d in range(1, n):
        to = (i + d) % n
        send(coup_ref.at[pl.ds(to * crow, crow)], cslots.at[d - 1], sum_s.at[d - 1], sum_r.at[d - 1], (to, j))
    exchanged(0)
    exchanged(1)
    emit(0, 1)
    emit(1, 1)
    gu[j] = up_ref[...]
    send(gu.at[j], gu.at[j], up_s.at[0], up_r.at[0], (i, across))
    send(gu.at[j], gu.at[j], up_s.at[1], up_r.at[1], (i, beside))
    for t in (0, 1):
        for k in (0, 1):
            advance(t, k, 1)
    pick_rows(i, vb_ref, piv_ref, pick_ref, mine)
    for t in (0, 1):
        for k in (0, 1):
            advance(t, k, 2)
    total = coup_ref[pl.ds(i * crow, crow), :]
    for d in range(1, n):
        receive(cslots.at[d - 1], sum_s.at[d - 1], sum_r.at[d - 1], ((i - d + n) % n, j))
        total = total + cslots[d - 1]
    gc[i, j] = total
    emit(2, 0)
    for t in (0, 1):
        for k in (0, 1):
            advance(t, k, 3)
    advance(2, 0, 1)
    for t in (0, 1):
        for k in (0, 1):
            advance(t, k, half)
    advance(2, 0, 2)
    crossed(0)
    for t in (0, 1):
        for k in (0, 1):
            side_arrivals(t, k)
    for d in range(1, n):
        to = (i + d) % n
        send(pick_ref.at[pl.ds(to * rows, rows)], xslots.at[d - 1], pick_s.at[d - 1], pick_r.at[d - 1], (to, j))
    assemble(n, m, gm, ge, uh, ul, lh, ll, bs)
    advance(2, 0, 3)
    crossed(1)
    receive(gu.at[across], up_s.at[0], up_r.at[0], (i, across))
    send(gu.at[across], gu.at[across], up_s.at[2], up_r.at[2], (i, beside))

    def service(p):
        if p == 1:
            advance(2, 0, half)
        if p in (2, 4, 6):
            crossed(p // 2 + 1)

    first_solve(bs, cs, wh, wl, uh, ul, service)
    own = pick_ref[pl.ds(i * rows, rows), :]
    for d in range(1, n):
        receive(xslots.at[d - 1], pick_s.at[d - 1], pick_r.at[d - 1], ((i - d + n) % n, j))
        own = own + xslots[d - 1]
    xparts[j] = own
    for d in range(1, m):
        send(xparts.at[j], xparts.at[j], x_s.at[d - 1], x_r.at[d - 1], (i, (j + d) % m))
    receive(gu.at[beside], up_s.at[1], up_r.at[1], (i, beside))
    receive(gu.at[guests[1]], up_s.at[2], up_r.at[2], (i, beside))
    rest_update(wh, wl, lambda ts: jnp.concatenate([gu[q, :, ts] for q in range(m)], axis=0), br_ref, wr_ref)
    for k in (0, 1):
        side_arrivals(2, k)
    for a in range(n):
        for b in range(m):
            cs[a * crow : (a + 1) * crow, b * cols : (b + 1) * cols] -= gc[a, b]
    second_solve(cs, wh, wl, lh, ll)
    interchange(i, wh, wl, vb_ref, piv_ref, xr_ref)
    for d in range(1, m):
        frm = (j - d + m) % m
        receive(xparts.at[frm], x_s.at[d - 1], x_r.at[d - 1], (i, frm))
    for q in range(m):
        xp[:, q * chunk : (q + 1) * chunk] = xparts[q]
    for cond, copy in pending:
        guard(cond, copy.wait_send)


def main_kernel(pre, g_ref, e_ref, c_ref, up_ref, br_ref, vb_ref, piv_ref, wr_ref, xr_ref, uh, ul, lh, ll, bs, cs, wh, wl):
    n_row, n_col, crow, cols = c_ref.shape
    assemble(n_row, n_col, g_ref, e_ref, uh, ul, lh, ll, bs)
    if not pre:
        for p in range(uh.shape[0] // BLOCK):
            sl = slice(p * BLOCK, (p + 1) * BLOCK)
            uh[sl, sl], ul[sl, sl] = split(inverse(uh[sl, sl].astype(F32) + ul[sl, sl].astype(F32), True))
            lh[sl, sl], ll[sl, sl] = split(inverse(lh[sl, sl].astype(F32) + ll[sl, sl].astype(F32), False))
    first_solve(bs, cs, wh, wl, uh, ul, lambda p: None)
    for a in range(n_row):
        for b in range(n_col):
            cs[a * crow : (a + 1) * crow, b * cols : (b + 1) * cols] -= c_ref[a, b]
    rest_update(wh, wl, lambda ts: up_ref[:, ts], br_ref, wr_ref)
    second_solve(cs, wh, wl, lh, ll)
    interchange(lax.axis_index("prow"), wh, wl, vb_ref, piv_ref, xr_ref)


def body(n_row, n_col, b_panel, b_rest, u_diag, u_panel, l_diag, l_below, v_below, pivot):
    rows, cols = u_diag.shape
    total, rhs = pivot.shape[0], b_panel.shape[1]
    chunk = rhs // n_col
    pre = rows == BLOCK
    piv = pivot[None, :]
    vm = pl.BlockSpec(memory_space=pltpu.VMEM)
    params = pltpu.CompilerParams(vmem_limit_bytes=56 << 20)
    halves = [pltpu.VMEM((total, total), BF16)] * 4
    halves += [pltpu.VMEM((total, rhs), F32), pltpu.VMEM((rhs, total), F32)]
    halves += [pltpu.VMEM((rhs, total), BF16)] * 2
    if pre and n_row == 8 and n_col == 4:
        crow, half = rhs // n_row, n_row // 2
        shapes = [(3, 2, 2, half), (3, 2, 2, half + 1), (2,), (n_row - 1,), (n_row - 1,), (n_col - 1,), (3,), (2, half + 1)]
        w_rest, x_rest, x_panel = pl.pallas_call(
            functools.partial(whole_kernel, n_row, n_col),
            out_shape=(
                jax.ShapeDtypeStruct(b_rest.shape, F32),
                jax.ShapeDtypeStruct(v_below.shape, F32),
                jax.ShapeDtypeStruct((rows, rhs), F32),
            ),
            in_specs=[vm] * 8,
            out_specs=(vm,) * 3,
            scratch_shapes=[
                pltpu.VMEM((n_row, n_col, rows, cols + chunk), F32),
                pltpu.VMEM((n_row, n_col, rows, cols), F32),
                pltpu.VMEM((n_row, n_col, crow, cols), F32),
                pltpu.VMEM((n_col,) + u_panel.shape, F32),
                pltpu.VMEM((rhs, cols), F32),
                pltpu.VMEM((total, chunk), F32),
            ]
            + halves
            + [
                pltpu.VMEM((n_row - 1, crow, cols), F32),
                pltpu.VMEM((n_row - 1, rows, chunk), F32),
                pltpu.VMEM((n_col, rows, chunk), F32),
            ]
            + [pltpu.SemaphoreType.DMA(shape) for shape in shapes for _ in range(2)],
            compiler_params=pltpu.CompilerParams(vmem_limit_bytes=60 << 20, collective_id=0, has_side_effects=True),
        )(u_diag, l_diag, b_panel, l_below, v_below, piv, u_panel, b_rest)
        return w_rest, x_panel, x_rest
    pack, extra, coup, pick = pl.pallas_call(
        functools.partial(prep_kernel, pre),
        out_shape=(
            jax.ShapeDtypeStruct((rows, cols + chunk), F32),
            jax.ShapeDtypeStruct((rows, cols), F32),
            jax.ShapeDtypeStruct((rhs, cols), F32),
            jax.ShapeDtypeStruct((total, chunk), F32),
        ),
        in_specs=[vm] * 6,
        out_specs=(vm,) * 4,
        compiler_params=params,
    )(u_diag, l_diag, b_panel, l_below, v_below, piv)

    def everywhere(piece):
        return lax.all_gather(piece, ("prow", "pcol"), axis=0).reshape((n_row, n_col) + piece.shape)

    upan = lax.all_gather(u_panel, "pcol", axis=0, tiled=True)
    csum = lax.psum_scatter(coup, "prow", scatter_dimension=0, tiled=True)
    xsum = lax.psum_scatter(pick, "prow", scatter_dimension=0, tiled=True)
    x_panel = lax.all_gather(xsum, "pcol", axis=1, tiled=True)
    w_rest, x_rest = pl.pallas_call(
        functools.partial(main_kernel, pre),
        out_shape=(jax.ShapeDtypeStruct(b_rest.shape, F32), jax.ShapeDtypeStruct(v_below.shape, F32)),
        in_specs=[vm] * 7,
        out_specs=(vm, vm),
        scratch_shapes=halves,
        compiler_params=params,
    )(everywhere(pack), everywhere(extra), everywhere(csum), upan, b_rest, v_below, piv)
    return w_rest, x_panel, x_rest


def solution(mesh):
    in_specs = (
        P("prow", None),
        P("prow", None),
        P("prow", "pcol"),
        P("pcol", "prow"),
        P("prow", "pcol"),
        P("prow", "pcol"),
        P("prow", None),
        P(),
    )
    out_specs = (P("prow", None), P("prow", None), P("prow", None))
    step = functools.partial(body, mesh.shape["prow"], mesh.shape["pcol"])
    return jax.shard_map(step, mesh=mesh, in_specs=in_specs, out_specs=out_specs, check_vma=False)
```
